32 devices in a mesh: row: 4 (over y, core), col: 8 (over z, x).
Axes of the slice: x: 2, y: 2, z: 4, core: 2. Of those that a mesh axis runs over, the one named last changes fastest.
Arguments:
- measured: float32 [1024, 3072], P('row', 'col'), may hold values from -32 to 32
- denoised: float32 [1024, 3072], P('row', 'col'), may hold values from -6 to 6
- reg_weight: float32 [1], replicated, may hold values from 0.5 to 2
- left_blocks: bfloat16 [2, 8, 3, 128, 128], replicated, may hold values from -0.3125 to 0.3125
- left_cols: int32 [2, 8, 3], replicated, may hold values from 0 to 7, as said below
- right_blocks: bfloat16 [2, 24, 3, 128, 128], replicated, may hold values from -0.3125 to 0.3125
- right_cols: int32 [2, 24, 3], replicated, may hold values from 0 to 23, as said below
Outputs:
- solution: float32 [1024, 3072], P('row', 'col')
- residual: float32 [1024, 3072], P('row', 'col')
The draws below stay inside these ranges and needn't reach their ends.
Inputs may be any that keep to these rules, and one draw needn't show every extreme that they name: `left_cols`: the three block columns of each block row of A_k are distinct and lie within 2 of that row's own block index. `right_cols`: the three block columns of each block row of B_k are distinct and lie within 2 of that row's own block index.
All inputs are finite; a program needn't handle non-finite values.
Results may differ from the reference program's by a relative error of at most 0.017.
Values may be sent and summed in bfloat16 or wider, within the bound.
A program may use at most 128 MiB of HBM per device.

```python
import math
import jax
import jax.numpy as jnp
from jax import lax

BLK = 128
ITERS = 2
NRB = 8
NCB = 24
NR = 1024
NC = 3072


def band_offsets(key, block_count):
    scores = jax.random.randint(key, (2, block_count, 5), 0, 4096) * 8 + jnp.arange(5, dtype=jnp.int32)
    row_ids = jnp.arange(block_count, dtype=jnp.int32)[None, :, None]
    target = row_ids + jnp.arange(5, dtype=jnp.int32) - 2
    inside = (target >= 0) & (target < block_count)
    scores = jnp.where(inside, scores, -1 - jnp.arange(5, dtype=jnp.int32))
    chosen, slot_ids = lax.top_k(scores, 3)
    return (row_ids + slot_ids - 2).astype(jnp.int32)


def draw_left_cols(key, part):
    return band_offsets(jax.random.fold_in(key, 11), NRB)


def draw_right_cols(key, part):
    return band_offsets(jax.random.fold_in(key, 12), NCB)


def draw_measured(key, part):
    key_rows, key_cols, key_base = jax.random.split(jax.random.fold_in(key, 13), 3)
    ramp = 0.6 + 1.2 * jnp.arange(NR, dtype=jnp.float32)[:, None] / NR
    row_scale = jnp.exp(jax.random.uniform(key_rows, (NR, 1), minval=-1.15, maxval=1.15))
    col_scale = jnp.exp(jax.random.uniform(key_cols, (1, NC), minval=-1.15, maxval=1.15))
    values = jnp.clip(jax.random.normal(key_base, (NR, NC)), -5.0, 5.0)
    return (0.35 * ramp * row_scale * col_scale * values).astype(jnp.float32)


def block_scale(key, extent, shards, low, high):
    def one(position, parts):
        heights = jax.random.uniform(jax.random.fold_in(jax.random.fold_in(key, 6), position), (parts,), jnp.float32, low / len(shards), high / len(shards))
        return jnp.repeat(jnp.exp(heights), extent[position] // parts).reshape((-1,) + (1,) * (len(extent) - position - 1))

    level = one(*shards[0])
    for cut in shards[1:]:
        level = level * one(*cut)
    return level


def normal_values(own_key, dims, deviation, reach, shards=(), kind=jnp.bfloat16):
    result = jax.random.normal(own_key, dims, jnp.float32) * deviation
    if len(shards) > 0:
        result = block_scale(own_key, dims, shards, -0.22, 0.18) * result
    return jnp.clip(result, min=-reach, max=reach).astype(kind)


def setup_inputs(seed: int = 0) -> dict:
    streams_of = jax.random.split(jax.random.key(seed), 8)
    measured = draw_measured(jax.random.fold_in(streams_of[7], 71), 0)
    denoised = normal_values(streams_of[1], (NR, NC), 1.0, 6.0, ((0, 4), (1, 8)), jnp.float32)
    reg_weight = jnp.clip(jnp.exp(jax.random.uniform(streams_of[2], (1,), jnp.float32, math.log(0.5), math.log(2.0))), 0.5, 2.0)
    left_blocks = normal_values(streams_of[3], (2, NRB, 3, BLK, BLK), (3 * BLK) ** -0.5, 0.3125)
    left_cols = draw_left_cols(jax.random.fold_in(streams_of[7], 71), 0)
    right_blocks = normal_values(streams_of[5], (2, NCB, 3, BLK, BLK), (3 * BLK) ** -0.5, 0.3125)
    right_cols = draw_right_cols(jax.random.fold_in(streams_of[7], 71), 0)
    return {"measured": measured, "denoised": denoised, "reg_weight": reg_weight, "left_blocks": left_blocks, "left_cols": left_cols, "right_blocks": right_blocks, "right_cols": right_cols}


def rows_forward(blocks, block_cols, source):
    block_count = blocks.shape[0]
    block_size = blocks.shape[2]
    field_width = source.shape[1]
    blocked = source.reshape(block_count, block_size, field_width)

    def one_row(row_index):
        running = jnp.zeros((block_size, field_width), jnp.float32)
        for slot_index in range(3):
            picked = lax.dynamic_index_in_dim(blocked, block_cols[row_index, slot_index], 0, keepdims=False)
            running = running + jnp.dot(blocks[row_index, slot_index], picked, preferred_element_type=jnp.float32)
        return running

    mapped = lax.map(one_row, jnp.arange(block_count, dtype=jnp.int32))
    return mapped.reshape(block_count * block_size, field_width)


def rows_adjoint(blocks, block_cols, source):
    block_count = blocks.shape[0]
    block_size = blocks.shape[2]
    field_width = source.shape[1]
    blocked = source.reshape(block_count, block_size, field_width)

    def add_row(running, row_index):
        picked = lax.dynamic_index_in_dim(blocked, row_index, 0, keepdims=False)
        for slot_index in range(3):
            term = jnp.dot(blocks[row_index, slot_index].T, picked, preferred_element_type=jnp.float32)
            target = block_cols[row_index, slot_index]
            current = lax.dynamic_index_in_dim(running, target, 0, keepdims=False)
            running = lax.dynamic_update_index_in_dim(running, current + term, target, 0)
        return running, None

    start = jnp.zeros((block_count, block_size, field_width), jnp.float32)
    running, unused = lax.scan(add_row, start, jnp.arange(block_count, dtype=jnp.int32))
    return running.reshape(block_count * block_size, field_width)


def forward_model(source, left_blocks, left_cols, right_blocks, right_cols):
    rounded = source.astype(jnp.bfloat16)
    running = jnp.zeros(source.shape, jnp.float32)
    for factor in range(2):
        inner = rows_forward(right_blocks[factor], right_cols[factor], rounded.T).T.astype(jnp.bfloat16)
        running = running + rows_forward(left_blocks[factor], left_cols[factor], inner)
    return running


def adjoint_model(source, left_blocks, left_cols, right_blocks, right_cols):
    rounded = source.astype(jnp.bfloat16)
    running = jnp.zeros(source.shape, jnp.float32)
    for factor in range(2):
        inner = rows_adjoint(left_blocks[factor], left_cols[factor], rounded).astype(jnp.bfloat16)
        running = running + rows_adjoint(right_blocks[factor], right_cols[factor], inner.T).T
    return lax.optimization_barrier(running.astype(jnp.bfloat16)).astype(jnp.float32)


def reference(measured, denoised, reg_weight, left_blocks, left_cols, right_blocks, right_cols):
    weight = reg_weight[0]

    def normal(source):
        forward = forward_model(source, left_blocks, left_cols, right_blocks, right_cols)
        return adjoint_model(forward, left_blocks, left_cols, right_blocks, right_cols) + weight * source

    rhs_field = adjoint_model(measured, left_blocks, left_cols, right_blocks, right_cols) + weight * denoised
    solution = jnp.zeros(measured.shape, jnp.float32)
    residual = rhs_field
    direction = rhs_field
    norm_now = jnp.sum(residual * residual)
    for iteration in range(ITERS):
        applied = normal(direction)
        step_size = norm_now / jnp.sum(direction * applied)
        solution = solution + step_size * direction
        residual = residual - step_size * applied
        if iteration + 1 < ITERS:
            norm_next = jnp.sum(residual * residual)
            direction = residual + (norm_next / (norm_now + 1e-6)) * direction
            norm_now = norm_next
    return solution, residual
```

```python
import functools

import jax
import jax.numpy as jnp
from jax import lax
from jax.experimental import pallas as pl
from jax.experimental.pallas import tpu as pltpu
from jax.sharding import PartitionSpec as P

MESH = pl.DeviceIdType.MESH
BF16 = jnp.bfloat16
F32 = jnp.float32
OPS = 5


def dot(a, b):
    return jnp.dot(a, b, preferred_element_type=F32)


def prep_kernel(
    own_rows, own_cols, block,
    lcols, rcols, lblk, rblk,
    bf_ref, ba_ref, af_ref, aa_ref,
    lwin, rwin, lsem, rsem,
):
    nrb, ncb = lblk.shape[1], rblk.shape[1]
    row0 = lax.axis_index("row") * own_rows - 2
    col0 = lax.axis_index("col") * own_cols - 2

    def fetch(source, window, sem, first, total, factor, slot):
        at = jnp.clip(first + slot, 0, total - 1)
        return pltpu.make_async_copy(
            source.at[factor, at], window.at[factor, slot], sem.at[factor, slot]
        )

    copies = []
    for factor in range(2):
        for slot in range(own_cols + 4):
            copies.append(fetch(rblk, rwin, rsem, col0, ncb, factor, slot))
        for slot in range(own_rows + 4):
            copies.append(fetch(lblk, lwin, lsem, row0, nrb, factor, slot))
    for copy in copies:
        copy.start()
    for ref in (bf_ref, ba_ref, af_ref, aa_ref):
        ref[...] = jnp.zeros_like(ref)
    for copy in copies:
        copy.wait()

    for factor in range(2):
        for slot in range(own_cols + 4):
            at = col0 + slot
            inside = (at >= 0) & (at < ncb)
            safe = jnp.clip(at, 0, ncb - 1)
            for j in range(3):
                target = rcols[factor, safe, j] - col0
                own = target - 2

                @pl.when(inside & (own >= 0) & (own < own_cols))
                def _(factor=factor, slot=slot, j=j, own=own):
                    lanes = pl.ds(pl.multiple_of(own * block, block), block)
                    ba_ref[factor, pl.ds(slot * block, block), lanes] = rwin[factor, slot, j]

                if 2 <= slot < own_cols + 2:
                    rows = pl.ds(pl.multiple_of(target * block, block), block)
                    bf_ref[factor, rows, pl.ds((slot - 2) * block, block)] = rwin[
                        factor, slot, j
                    ].T
        for slot in range(own_rows + 4):
            at = row0 + slot
            inside = (at >= 0) & (at < nrb)
            safe = jnp.clip(at, 0, nrb - 1)
            for j in range(3):
                target = lcols[factor, safe, j] - row0
                own = target - 2

                @pl.when(inside & (own >= 0) & (own < own_rows))
                def _(factor=factor, slot=slot, j=j, own=own):
                    rows = pl.ds(pl.multiple_of(own * block, block), block)
                    aa_ref[factor, rows, pl.ds(slot * block, block)] = lwin[factor, slot, j].T

                if 2 <= slot < own_rows + 2:
                    lanes = pl.ds(pl.multiple_of(target * block, block), block)
                    af_ref[factor, pl.ds((slot - 2) * block, block), lanes] = lwin[
                        factor, slot, j
                    ]


def main_kernel(
    nrow, ncol, halo,
    weight_ref, meas_ref, den_ref, bf_ref, ba_ref, af_ref, aa_ref,
    sol_ref, res_ref,
    xo, xl, xr, wo, wu, wd, v0, v1, v2, stat, rstat, cstat,
    xsend, xrecv, wsend, wrecv, rsend, rrecv, csend, crecv,
):
    row = lax.axis_index("row")
    col = lax.axis_index("col")
    height, width = meas_ref.shape
    has_left, has_right = col > 0, col < ncol - 1
    has_up, has_down = row > 0, row < nrow - 1
    left, right = jnp.maximum(col - 1, 0), jnp.minimum(col + 1, ncol - 1)
    up, down = jnp.maximum(row - 1, 0), jnp.minimum(row + 1, nrow - 1)

    @pl.when(jnp.logical_not(has_left))
    def _():
        xl[...] = jnp.zeros_like(xl)

    @pl.when(jnp.logical_not(has_right))
    def _():
        xr[...] = jnp.zeros_like(xr)

    @pl.when(jnp.logical_not(has_up))
    def _():
        wu[...] = jnp.zeros_like(wu)

    @pl.when(jnp.logical_not(has_down))
    def _():
        wd[...] = jnp.zeros_like(wd)

    barrier = pltpu.get_barrier_semaphore()
    for step in range(1, nrow):
        pl.semaphore_signal(
            barrier, inc=1, device_id=(lax.rem(row + step, nrow), col), device_id_type=MESH
        )
    for step in range(1, ncol):
        pl.semaphore_signal(
            barrier, inc=1, device_id=(row, lax.rem(col + step, ncol)), device_id_type=MESH
        )
    pl.semaphore_wait(barrier, nrow + ncol - 2)

    def remote(src, dst, send, recv, device):
        return pltpu.make_async_remote_copy(
            src_ref=src, dst_ref=dst, send_sem=send, recv_sem=recv,
            device_id=device, device_id_type=MESH,
        )

    pending = []

    def operate(index, bmat, amat):
        to_right = remote(
            xo.at[index, :, pl.ds(width - halo, halo)], xl.at[index],
            xsend.at[index, 0], xrecv.at[index, 0], (row, right),
        )
        to_left = remote(
            xo.at[index, :, pl.ds(0, halo)], xr.at[index],
            xsend.at[index, 1], xrecv.at[index, 1], (row, left),
        )
        pl.when(has_right)(to_right.start)
        pl.when(has_left)(to_left.start)
        pending.append((has_right, to_right))
        pending.append((has_left, to_left))
        acc = [dot(xo[index], bmat[k, pl.ds(halo, width), :]) for k in range(2)]
        pl.when(has_left)(to_right.wait_recv)
        pl.when(has_right)(to_left.wait_recv)
        for k in range(2):
            total = acc[k] + dot(xl[index], bmat[k, pl.ds(0, halo), :])
            total = total + dot(xr[index], bmat[k, pl.ds(halo + width, halo), :])
            wo[index, k] = total.astype(BF16)
        to_down = remote(
            wo.at[index], wu.at[index], wsend.at[index, 0], wrecv.at[index, 0], (down, col)
        )
        to_up = remote(
            wo.at[index], wd.at[index], wsend.at[index, 1], wrecv.at[index, 1], (up, col)
        )
        pl.when(has_down)(to_down.start)
        pl.when(has_up)(to_up.start)
        pending.append((has_down, to_down))
        pending.append((has_up, to_up))
        out = dot(amat[0, :, pl.ds(halo, height)], wo[index, 0])
        out = out + dot(amat[1, :, pl.ds(halo, height)], wo[index, 1])
        pl.when(has_up)(to_down.wait_recv)
        pl.when(has_down)(to_up.wait_recv)
        for k in range(2):
            out = out + dot(amat[k, :, pl.ds(0, halo)], wu[index, k])
            out = out + dot(amat[k, :, pl.ds(halo + height, halo)], wd[index, k])
        return out

    weight = weight_ref[0]
    xo[0] = meas_ref[...].astype(BF16)
    first = operate(0, ba_ref, aa_ref) + weight * den_ref[...]
    v0[...] = first
    xo[1] = first.astype(BF16)
    xo[2] = operate(1, bf_ref, af_ref).astype(BF16)
    second = operate(2, ba_ref, aa_ref) + weight * v0[...]
    v1[...] = second
    xo[3] = second.astype(BF16)
    xo[4] = operate(3, bf_ref, af_ref).astype(BF16)
    v2[...] = operate(4, ba_ref, aa_ref) + weight * v1[...]

    def lanes(a, b):
        folded = jnp.sum(a[...] * b[...], axis=0, keepdims=True)
        total = folded[:, 0:128]
        for start in range(128, width, 128):
            total = total + folded[:, start : start + 128]
        return total

    for slot, (a, b) in enumerate(((v0, v0), (v0, v1), (v1, v1), (v0, v2), (v1, v2))):
        stat[0, pl.ds(slot, 1), :] = lanes(a, b)
    stat[0, pl.ds(5, 3), :] = jnp.zeros((3, 128), F32)

    def gather(source, slots, send, recv, count, device):
        copies = [
            remote(source, slots.at[step - 1], send.at[step - 1], recv.at[step - 1], device(step))
            for step in range(1, count)
        ]
        for copy in copies:
            copy.start()
        for copy in copies:
            copy.wait_recv()
        total = source[...]
        for step in range(1, count):
            total = total + slots[step - 1]
        for copy in copies:
            copy.wait_send()
        return total

    stat[1] = gather(
        stat.at[0], rstat, rsend, rrecv, nrow, lambda step: (lax.rem(row + step, nrow), col)
    )
    summed = gather(
        stat.at[1], cstat, csend, crecv, ncol, lambda step: (row, lax.rem(col + step, ncol))
    )
    grams = jnp.sum(summed, axis=1, keepdims=True)
    g00, g01, g11, g02, g12 = [grams[slot : slot + 1, :] for slot in range(5)]
    alpha = g00 / g01
    norm = alpha * alpha * g11 - 2.0 * alpha * g01 + g00
    beta = norm / (g00 + 1e-06)
    grow = 1.0 + beta
    curve = grow * grow * g01 - grow * alpha * (g02 + g11) + alpha * alpha * g12
    gamma = norm / curve
    sol_ref[...] = (alpha + gamma * grow) * v0[...] - (gamma * alpha) * v1[...]
    res_ref[...] = (
        v0[...] - (alpha + gamma * grow) * v1[...] + (gamma * alpha) * v2[...]
    )
    for condition, copy in pending:
        pl.when(condition)(copy.wait_send)


def shards(measured, denoised, reg_weight, left_blocks, left_cols, right_blocks, right_cols):
    block = left_blocks.shape[-1]
    height, width = measured.shape
    own_rows, own_cols = height // block, width // block
    nrow, ncol = lax.axis_size("row"), lax.axis_size("col")
    halo = 2 * block
    vmem = pl.BlockSpec(memory_space=pltpu.VMEM)
    smem = pl.BlockSpec(memory_space=pltpu.SMEM)
    hbm = pl.BlockSpec(memory_space=pl.ANY)
    wide, tall = width + 2 * halo, height + 2 * halo

    bf, ba, af, aa = pl.pallas_call(
        functools.partial(prep_kernel, own_rows, own_cols, block),
        out_shape=[
            jax.ShapeDtypeStruct((2, wide, width), BF16),
            jax.ShapeDtypeStruct((2, wide, width), BF16),
            jax.ShapeDtypeStruct((2, height, tall), BF16),
            jax.ShapeDtypeStruct((2, height, tall), BF16),
        ],
        in_specs=[smem, smem, hbm, hbm],
        out_specs=[vmem] * 4,
        scratch_shapes=[
            pltpu.VMEM((2, own_rows + 4, 3, block, block), BF16),
            pltpu.VMEM((2, own_cols + 4, 3, block, block), BF16),
            pltpu.SemaphoreType.DMA((2, own_rows + 4)),
            pltpu.SemaphoreType.DMA((2, own_cols + 4)),
        ],
        name="windows",
    )(left_cols, right_cols, left_blocks, right_blocks)

    dma = pltpu.SemaphoreType.DMA
    return pl.pallas_call(
        functools.partial(main_kernel, nrow, ncol, halo),
        out_shape=[jax.ShapeDtypeStruct((height, width), F32)] * 2,
        in_specs=[smem] + [vmem] * 6,
        out_specs=[vmem] * 2,
        scratch_shapes=[
            pltpu.VMEM((OPS, height, width), BF16),
            pltpu.VMEM((OPS, height, halo), BF16),
            pltpu.VMEM((OPS, height, halo), BF16),
            pltpu.VMEM((OPS, 2, height, width), BF16),
            pltpu.VMEM((OPS, 2, halo, width), BF16),
            pltpu.VMEM((OPS, 2, halo, width), BF16),
            pltpu.VMEM((height, width), F32),
            pltpu.VMEM((height, width), F32),
            pltpu.VMEM((height, width), F32),
            pltpu.VMEM((2, 8, 128), F32),
            pltpu.VMEM((nrow - 1, 8, 128), F32),
            pltpu.VMEM((ncol - 1, 8, 128), F32),
            dma((OPS, 2)), dma((OPS, 2)), dma((OPS, 2)), dma((OPS, 2)),
            dma((nrow - 1,)), dma((nrow - 1,)), dma((ncol - 1,)), dma((ncol - 1,)),
        ],
        compiler_params=pltpu.CompilerParams(
            collective_id=0, has_side_effects=True, vmem_limit_bytes=48 * 1024 * 1024
        ),
        name="conjugate",
    )(reg_weight, measured, denoised, bf, ba, af, aa)


def solution(mesh):
    return jax.shard_map(
        shards,
        mesh=mesh,
        in_specs=(P("row", "col"), P("row", "col"), P(), P(), P(), P(), P()),
        out_specs=(P("row", "col"), P("row", "col")),
        check_vma=False,
    )
```

```python
import functools

import jax
import jax.numpy as jnp
from jax import lax
from jax.experimental import pallas as pl
from jax.experimental.pallas import tpu as pltpu
from jax.sharding import PartitionSpec as P

MESH = pl.DeviceIdType.MESH
BF16 = jnp.bfloat16
F32 = jnp.float32
OPS = 5


def dot(a, b):
    return jnp.dot(a, b, preferred_element_type=F32)


def main_kernel(
    nrow, ncol, block,
    weight_ref, lcols, rcols, meas_hbm, den_hbm, lblk, rblk,
    sol_ref, res_ref,
    meas, den, lwin, rwin, bf_ref, ba_ref, af_ref, aa_ref,
    xo, xl, xr, wo, wu, wd, v0, v1, v2, stat, rstat, cstat,
    msem, lsem, rsem, xsend, xrecv, wsend, wrecv, rsend, rrecv, csend, crecv,
):
    row = lax.axis_index("row")
    col = lax.axis_index("col")
    height, width = meas.shape
    halo = 2 * block
    own_rows, own_cols = height // block, width // block
    nrb, ncb = lblk.shape[1], rblk.shape[1]
    row0, col0 = row * own_rows - 2, col * own_cols - 2
    has_left, has_right = col > 0, col < ncol - 1
    has_up, has_down = row > 0, row < nrow - 1
    left, right = jnp.maximum(col - 1, 0), jnp.minimum(col + 1, ncol - 1)
    up, down = jnp.maximum(row - 1, 0), jnp.minimum(row + 1, nrow - 1)

    load_meas = pltpu.make_async_copy(meas_hbm, meas, msem.at[0])
    load_den = pltpu.make_async_copy(den_hbm, den, msem.at[1])
    load_meas.start()

    def fetch(source, window, sem, first, total, count):
        return [
            pltpu.make_async_copy(
                source.at[k, jnp.clip(first + t, 0, total - 1)], window.at[k, t], sem.at[k, t]
            )
            for k in range(2)
            for t in range(count)
        ]

    load_right = fetch(rblk, rwin, rsem, col0, ncb, own_cols + 4)
    load_left = fetch(lblk, lwin, lsem, row0, nrb, own_rows + 4)
    for copy in load_right:
        copy.start()
    for copy in load_left:
        copy.start()
    load_den.start()

    barrier = pltpu.get_barrier_semaphore()

    @pl.when(jnp.logical_not(has_left))
    def _():
        xl[...] = jnp.zeros_like(xl)

    @pl.when(jnp.logical_not(has_right))
    def _():
        xr[...] = jnp.zeros_like(xr)

    @pl.when(jnp.logical_not(has_up))
    def _():
        wu[...] = jnp.zeros_like(wu)

    @pl.when(jnp.logical_not(has_down))
    def _():
        wd[...] = jnp.zeros_like(wd)

    for step in range(1, nrow):
        pl.semaphore_signal(
            barrier, inc=1, device_id=(lax.rem(row + step, nrow), col), device_id_type=MESH
        )
    for step in range(1, ncol):
        pl.semaphore_signal(
            barrier, inc=1, device_id=(row, lax.rem(col + step, ncol)), device_id_type=MESH
        )
    load_meas.wait()
    xo[0] = meas[...].astype(BF16)
    pl.semaphore_wait(barrier, nrow + ncol - 2)

    def remote(src, dst, send, recv, device):
        return pltpu.make_async_remote_copy(
            src_ref=src, dst_ref=dst, send_sem=send, recv_sem=recv,
            device_id=device, device_id_type=MESH,
        )

    def hit(cols, k, at, total, j, wanted):
        inside = (at >= 0) & (at < total)
        same = cols[k, jnp.clip(at, 0, total - 1), j] == wanted
        return jnp.where(inside & same, 1.0, 0.0).astype(F32)

    def mixed(sources, weights):
        total = sources[0] * weights[0]
        for source, factor in zip(sources[1:], weights[1:]):
            total = total + source * factor
        return total

    def span(index):
        return pl.ds(index * block, block)

    empty = jnp.zeros((block, block), BF16)

    def build_ba():
        for copy in load_right:
            copy.wait()
        for k in range(2):
            for t in range(own_cols + 4):
                sources = [rwin[k, t, j].astype(F32) for j in range(3)]
                for c in range(own_cols):
                    if c <= t <= c + 4:
                        weights = [
                            hit(rcols, k, col0 + t, ncb, j, col0 + 2 + c) for j in range(3)
                        ]
                        ba_ref[k, span(t), span(c)] = mixed(sources, weights).astype(BF16)
                    else:
                        ba_ref[k, span(t), span(c)] = empty

    def build_bf():
        for k in range(2):
            for c in range(own_cols):
                sources = [rwin[k, c + 2, j].astype(F32).T for j in range(3)]
                for t in range(own_cols + 4):
                    if c <= t <= c + 4:
                        weights = [
                            hit(rcols, k, col0 + 2 + c, ncb, j, col0 + t) for j in range(3)
                        ]
                        bf_ref[k, span(t), span(c)] = mixed(sources, weights).astype(BF16)
                    else:
                        bf_ref[k, span(t), span(c)] = empty

    def build_aa():
        for copy in load_left:
            copy.wait()
        for k in range(2):
            for t in range(own_rows + 4):
                sources = [lwin[k, t, j].astype(F32) for j in range(3)]
                for r in range(own_rows):
                    if r <= t <= r + 4:
                        weights = [
                            hit(lcols, k, row0 + t, nrb, j, row0 + 2 + r) for j in range(3)
                        ]
                        aa_ref[k, span(r), span(t)] = mixed(sources, weights).T.astype(BF16)
                    else:
                        aa_ref[k, span(r), span(t)] = empty

    def build_af():
        for k in range(2):
            for r in range(own_rows):
                sources = [lwin[k, r + 2, j].astype(F32) for j in range(3)]
                for t in range(own_rows + 4):
                    if r <= t <= r + 4:
                        weights = [
                            hit(lcols, k, row0 + 2 + r, nrb, j, row0 + t) for j in range(3)
                        ]
                        af_ref[k, span(r), span(t)] = mixed(sources, weights).astype(BF16)
                    else:
                        af_ref[k, span(r), span(t)] = empty

    pending = []
    chunks = range(own_rows)

    def operate(index, bmat, amat, fill_b=None, fill_a=None):
        sides = []
        for q in chunks:
            to_right = remote(
                xo.at[index, span(q), pl.ds(width - halo, halo)], xl.at[index, span(q)],
                xsend.at[index, q, 0], xrecv.at[index, q, 0], (row, right),
            )
            to_left = remote(
                xo.at[index, span(q), pl.ds(0, halo)], xr.at[index, span(q)],
                xsend.at[index, q, 1], xrecv.at[index, q, 1], (row, left),
            )
            pl.when(has_right)(to_right.start)
            pl.when(has_left)(to_left.start)
            pending.append((has_right, to_right))
            pending.append((has_left, to_left))
            sides.append((to_right, to_left))
        if fill_b is not None:
            fill_b()
        acc = [dot(xo[index], bmat[k, pl.ds(halo, width), :]) for k in range(2)]
        ends = []
        for q in chunks:
            to_right, to_left = sides[q]
            pl.when(has_left)(to_right.wait_recv)
            pl.when(has_right)(to_left.wait_recv)
            for k in range(2):
                total = acc[k][q * block : (q + 1) * block]
                total = total + dot(xl[index, span(q)], bmat[k, pl.ds(0, halo), :])
                total = total + dot(xr[index, span(q)], bmat[k, pl.ds(halo + width, halo), :])
                wo[index, q, k] = total.astype(BF16)
            to_down = remote(
                wo.at[index, q], wu.at[index, q],
                wsend.at[index, q, 0], wrecv.at[index, q, 0], (down, col),
            )
            to_up = remote(
                wo.at[index, q], wd.at[index, q],
                wsend.at[index, q, 1], wrecv.at[index, q, 1], (up, col),
            )
            pl.when(has_down)(to_down.start)
            pl.when(has_up)(to_up.start)
            pending.append((has_down, to_down))
            pending.append((has_up, to_up))
            ends.append((to_down, to_up))
        if fill_a is not None:
            fill_a()

        def part(products, first):
            sums = [
                dot(
                    amat[k, :, pl.ds(first * block, height)],
                    jnp.concatenate([products[index, q, k] for q in chunks], axis=0),
                )
                for k in range(2)
            ]
            return sums[0] + sums[1]

        out = part(wo, 2)
        for q in chunks:
            to_down, to_up = ends[q]
            pl.when(has_up)(to_down.wait_recv)
            pl.when(has_down)(to_up.wait_recv)
        return out + part(wu, 0) + part(wd, 2 + own_rows)

    weight = weight_ref[0]
    first = operate(0, ba_ref, aa_ref, build_ba, build_aa)
    load_den.wait()
    first = first + weight * den[...]
    xo[1] = first.astype(BF16)
    v0[...] = first
    xo[2] = operate(1, bf_ref, af_ref, build_bf, build_af).astype(BF16)
    second = operate(2, ba_ref, aa_ref) + weight * v0[...]
    xo[3] = second.astype(BF16)
    v1[...] = second
    xo[4] = operate(3, bf_ref, af_ref).astype(BF16)
    v2[...] = operate(4, ba_ref, aa_ref) + weight * v1[...]

    def lanes(a, b):
        folded = jnp.sum(a[...] * b[...], axis=0, keepdims=True)
        total = folded[:, 0:128]
        for start in range(128, width, 128):
            total = total + folded[:, start : start + 128]
        return total

    for slot, (a, b) in enumerate(((v0, v0), (v0, v1), (v1, v1), (v0, v2), (v1, v2))):
        stat[0, pl.ds(slot, 1), :] = lanes(a, b)
    stat[0, pl.ds(5, 3), :] = jnp.zeros((3, 128), F32)

    def gather(source, slots, send, recv, count, device):
        copies = [
            remote(source, slots.at[step - 1], send.at[step - 1], recv.at[step - 1], device(step))
            for step in range(1, count)
        ]
        for copy in copies:
            copy.start()
        for copy in copies:
            copy.wait_recv()
        total = source[...]
        for step in range(1, count):
            total = total + slots[step - 1]
        for copy in copies:
            copy.wait_send()
        return total

    stat[1] = gather(
        stat.at[0], rstat, rsend, rrecv, nrow, lambda step: (lax.rem(row + step, nrow), col)
    )
    summed = gather(
        stat.at[1], cstat, csend, crecv, ncol, lambda step: (row, lax.rem(col + step, ncol))
    )
    grams = jnp.sum(summed, axis=1, keepdims=True)
    g00, g01, g11, g02, g12 = [grams[slot : slot + 1, :] for slot in range(5)]
    alpha = g00 / g01
    norm = alpha * alpha * g11 - 2.0 * alpha * g01 + g00
    beta = norm / (g00 + 1e-06)
    grow = 1.0 + beta
    curve = grow * grow * g01 - grow * alpha * (g02 + g11) + alpha * alpha * g12
    gamma = norm / curve
    sol_ref[...] = (alpha + gamma * grow) * v0[...] - (gamma * alpha) * v1[...]
    res_ref[...] = (
        v0[...] - (alpha + gamma * grow) * v1[...] + (gamma * alpha) * v2[...]
    )
    for condition, copy in pending:
        pl.when(condition)(copy.wait_send)


def shards(measured, denoised, reg_weight, left_blocks, left_cols, right_blocks, right_cols):
    block = left_blocks.shape[-1]
    height, width = measured.shape
    own_rows, own_cols = height // block, width // block
    nrow, ncol = lax.axis_size("row"), lax.axis_size("col")
    halo = 2 * block
    smem = pl.BlockSpec(memory_space=pltpu.SMEM)
    hbm = pl.BlockSpec(memory_space=pl.ANY)
    wide, tall = width + 2 * halo, height + 2 * halo
    field = pltpu.VMEM((height, width), F32)
    dma = pltpu.SemaphoreType.DMA
    return pl.pallas_call(
        functools.partial(main_kernel, nrow, ncol, block),
        out_shape=[jax.ShapeDtypeStruct((height, width), F32)] * 2,
        in_specs=[smem] * 3 + [hbm] * 4,
        out_specs=[pl.BlockSpec(memory_space=pltpu.VMEM)] * 2,
        scratch_shapes=[
            field,
            field,
            pltpu.VMEM((2, own_rows + 4, 3, block, block), BF16),
            pltpu.VMEM((2, own_cols + 4, 3, block, block), BF16),
            pltpu.VMEM((2, wide, width), BF16),
            pltpu.VMEM((2, wide, width), BF16),
            pltpu.VMEM((2, height, tall), BF16),
            pltpu.VMEM((2, height, tall), BF16),
            pltpu.VMEM((OPS, height, width), BF16),
            pltpu.VMEM((OPS, height, halo), BF16),
            pltpu.VMEM((OPS, height, halo), BF16),
            pltpu.VMEM((OPS, own_rows, 2, block, width), BF16),
            pltpu.VMEM((OPS, own_rows, 2, block, width), BF16),
            pltpu.VMEM((OPS, own_rows, 2, block, width), BF16),
            field,
            field,
            field,
            pltpu.VMEM((2, 8, 128), F32),
            pltpu.VMEM((nrow - 1, 8, 128), F32),
            pltpu.VMEM((ncol - 1, 8, 128), F32),
            dma((2,)), dma((2, own_rows + 4)), dma((2, own_cols + 4)),
            dma((OPS, own_rows, 2)), dma((OPS, own_rows, 2)),
            dma((OPS, own_rows, 2)), dma((OPS, own_rows, 2)),
            dma((nrow - 1,)), dma((nrow - 1,)), dma((ncol - 1,)), dma((ncol - 1,)),
        ],
        compiler_params=pltpu.CompilerParams(
            collective_id=0, has_side_effects=True, vmem_limit_bytes=48 * 1024 * 1024
        ),
        name="conjugate",
    )(reg_weight, left_cols, right_cols, measured, denoised, left_blocks, right_blocks)


def solution(mesh):
    return jax.shard_map(
        shards,
        mesh=mesh,
        in_specs=(P("row", "col"), P("row", "col"), P(), P(), P(), P(), P()),
        out_specs=(P("row", "col"), P("row", "col")),
        check_vma=False,
    )
```

```python
import functools

import jax
import jax.numpy as jnp
from jax import lax
from jax.experimental import pallas as pl
from jax.experimental.pallas import tpu as pltpu
from jax.sharding import PartitionSpec as P

MESH = pl.DeviceIdType.MESH
BF16 = jnp.bfloat16
F32 = jnp.float32
OPS = 5


def dot(a, b):
    return jnp.dot(a, b, preferred_element_type=F32)


def main_kernel(
    nrow, ncol, block,
    weight_ref, lcols, rcols, meas_hbm, den_hbm, lblk, rblk,
    sol_ref, res_ref,
    meas, den, lwin, rwin, bf_ref, ba_ref, af_ref, aa_ref,
    xo, xl, xr, wo, pu, pd, ru, rd, v0, v1, v2, stat, rstat, cstat,
    msem, lsem, rsem, xsend, xrecv, wsend, wrecv, rsend, rrecv, csend, crecv,
):
    row = lax.axis_index("row")
    col = lax.axis_index("col")
    height, width = meas.shape
    halo = 2 * block
    own_rows, own_cols = height // block, width // block
    nrb, ncb = lblk.shape[1], rblk.shape[1]
    row0, col0 = row * own_rows - 2, col * own_cols - 2
    has_left, has_right = col > 0, col < ncol - 1
    has_up, has_down = row > 0, row < nrow - 1
    left, right = jnp.maximum(col - 1, 0), jnp.minimum(col + 1, ncol - 1)
    up, down = jnp.maximum(row - 1, 0), jnp.minimum(row + 1, nrow - 1)

    load_meas = pltpu.make_async_copy(meas_hbm, meas, msem.at[0])
    load_den = pltpu.make_async_copy(den_hbm, den, msem.at[1])
    load_meas.start()

    def fetch(source, window, sem, first, total, count):
        return [
            pltpu.make_async_copy(
                source.at[k, jnp.clip(first + t, 0, total - 1)], window.at[k, t], sem.at[k, t]
            )
            for k in range(2)
            for t in range(count)
        ]

    load_right = fetch(rblk, rwin, rsem, col0, ncb, own_cols + 4)
    load_left = fetch(lblk, lwin, lsem, row0, nrb, own_rows + 4)
    for copy in load_right:
        copy.start()
    for copy in load_left:
        copy.start()
    load_den.start()

    barrier = pltpu.get_barrier_semaphore()

    @pl.when(jnp.logical_not(has_left))
    def _():
        xl[...] = jnp.zeros_like(xl)

    @pl.when(jnp.logical_not(has_right))
    def _():
        xr[...] = jnp.zeros_like(xr)

    @pl.when(jnp.logical_not(has_up))
    def _():
        ru[...] = jnp.zeros_like(ru)

    @pl.when(jnp.logical_not(has_down))
    def _():
        rd[...] = jnp.zeros_like(rd)

    for step in range(1, nrow):
        pl.semaphore_signal(
            barrier, inc=1, device_id=(lax.rem(row + step, nrow), col), device_id_type=MESH
        )
    for step in range(1, ncol):
        pl.semaphore_signal(
            barrier, inc=1, device_id=(row, lax.rem(col + step, ncol)), device_id_type=MESH
        )
    load_meas.wait()
    xo[0] = meas[...].astype(BF16)
    pl.semaphore_wait(barrier, nrow + ncol - 2)

    def remote(src, dst, send, recv, device):
        return pltpu.make_async_remote_copy(
            src_ref=src, dst_ref=dst, send_sem=send, recv_sem=recv,
            device_id=device, device_id_type=MESH,
        )

    def hit(cols, k, at, total, j, wanted):
        inside = (at >= 0) & (at < total)
        same = cols[k, jnp.clip(at, 0, total - 1), j] == wanted
        return jnp.where(inside & same, 1.0, 0.0).astype(F32)

    def mixed(sources, weights):
        total = sources[0] * weights[0]
        for source, factor in zip(sources[1:], weights[1:]):
            total = total + source * factor
        return total

    def span(index):
        return pl.ds(index * block, block)

    empty = jnp.zeros((block, block), BF16)

    def build_ba():
        for copy in load_right:
            copy.wait()
        for k in range(2):
            for t in range(own_cols + 4):
                sources = [rwin[k, t, j].astype(F32) for j in range(3)]
                for c in range(own_cols):
                    if c <= t <= c + 4:
                        weights = [
                            hit(rcols, k, col0 + t, ncb, j, col0 + 2 + c) for j in range(3)
                        ]
                        ba_ref[k, span(t), span(c)] = mixed(sources, weights).astype(BF16)
                    else:
                        ba_ref[k, span(t), span(c)] = empty

    def build_bf():
        for k in range(2):
            for c in range(own_cols):
                sources = [rwin[k, c + 2, j].astype(F32).T for j in range(3)]
                for t in range(own_cols + 4):
                    if c <= t <= c + 4:
                        weights = [
                            hit(rcols, k, col0 + 2 + c, ncb, j, col0 + t) for j in range(3)
                        ]
                        bf_ref[k, span(t), span(c)] = mixed(sources, weights).astype(BF16)
                    else:
                        bf_ref[k, span(t), span(c)] = empty

    def build_aa():
        for copy in load_left:
            copy.wait()
        for k in range(2):
            for r in range(own_rows):
                sources = [lwin[k, r + 2, j].astype(F32).T for j in range(3)]
                for t in range(own_rows + 4):
                    if r <= t <= r + 4:
                        weights = [
                            hit(lcols, k, row0 + 2 + r, nrb, j, row0 + t) for j in range(3)
                        ]
                        value = mixed(sources, weights).astype(BF16)
                    else:
                        value = empty
                    aa_ref[span(t), span(k * own_rows + r)] = value

    def build_af():
        for k in range(2):
            for t in range(own_rows + 4):
                sources = [lwin[k, t, j].astype(F32) for j in range(3)]
                for r in range(own_rows):
                    if r <= t <= r + 4:
                        weights = [
                            hit(lcols, k, row0 + t, nrb, j, row0 + 2 + r) for j in range(3)
                        ]
                        value = mixed(sources, weights).astype(BF16)
                    else:
                        value = empty
                    af_ref[span(t), span(k * own_rows + r)] = value

    pending = []
    chunks = range(own_rows)

    def operate(index, bmat, amat, fill_b=None, fill_a=None):
        sides = []
        for q in chunks:
            to_right = remote(
                xo.at[index, span(q), pl.ds(width - halo, halo)], xl.at[index, span(q)],
                xsend.at[index, q, 0], xrecv.at[index, q, 0], (row, right),
            )
            to_left = remote(
                xo.at[index, span(q), pl.ds(0, halo)], xr.at[index, span(q)],
                xsend.at[index, q, 1], xrecv.at[index, q, 1], (row, left),
            )
            pl.when(has_right)(to_right.start)
            pl.when(has_left)(to_left.start)
            pending.append((has_right, to_right))
            pending.append((has_left, to_left))
            sides.append((to_right, to_left))
        if fill_b is not None:
            fill_b()
        acc = [dot(xo[index], bmat[k, pl.ds(halo, width), :]) for k in range(2)]
        for q in chunks:
            to_right, to_left = sides[q]
            pl.when(has_left)(to_right.wait_recv)
            pl.when(has_right)(to_left.wait_recv)
            for k in range(2):
                total = acc[k][q * block : (q + 1) * block]
                total = total + dot(xl[index, span(q)], bmat[k, pl.ds(0, halo), :])
                total = total + dot(xr[index, span(q)], bmat[k, pl.ds(halo + width, halo), :])
                wo[span(k * own_rows + q)] = total.astype(BF16)
        if fill_a is not None:
            fill_a()
        products = wo[...]
        to_down = remote(
            pd.at[index], ru.at[index], wsend.at[index, 0], wrecv.at[index, 0], (down, col)
        )
        to_up = remote(
            pu.at[index], rd.at[index], wsend.at[index, 1], wrecv.at[index, 1], (up, col)
        )
        pd[index] = dot(amat[pl.ds(halo + height, halo), :], products).astype(BF16)
        pl.when(has_down)(to_down.start)
        pu[index] = dot(amat[pl.ds(0, halo), :], products).astype(BF16)
        pl.when(has_up)(to_up.start)
        pending.append((has_down, to_down))
        pending.append((has_up, to_up))
        out = dot(amat[pl.ds(halo, height), :], products)
        pl.when(has_up)(to_down.wait_recv)
        pl.when(has_down)(to_up.wait_recv)
        return out + ru[index].astype(F32) + rd[index].astype(F32)

    weight = weight_ref[0]
    first = operate(0, ba_ref, aa_ref, build_ba, build_aa)
    load_den.wait()
    first = first + weight * den[...]
    xo[1] = first.astype(BF16)
    v0[...] = first
    xo[2] = operate(1, bf_ref, af_ref, build_bf, build_af).astype(BF16)
    second = operate(2, ba_ref, aa_ref) + weight * v0[...]
    xo[3] = second.astype(BF16)
    v1[...] = second
    xo[4] = operate(3, bf_ref, af_ref).astype(BF16)
    v2[...] = operate(4, ba_ref, aa_ref) + weight * v1[...]

    def lanes(a, b):
        folded = jnp.sum(a[...] * b[...], axis=0, keepdims=True)
        total = folded[:, 0:128]
        for start in range(128, width, 128):
            total = total + folded[:, start : start + 128]
        return total

    for slot, (a, b) in enumerate(((v0, v0), (v0, v1), (v1, v1), (v0, v2), (v1, v2))):
        stat[0, pl.ds(slot, 1), :] = lanes(a, b)
    stat[0, pl.ds(5, 3), :] = jnp.zeros((3, 128), F32)

    def gather(source, slots, send, recv, count, device):
        copies = [
            remote(source, slots.at[step - 1], send.at[step - 1], recv.at[step - 1], device(step))
            for step in range(1, count)
        ]
        for copy in copies:
            copy.start()
        for copy in copies:
            copy.wait_recv()
        total = source[...]
        for step in range(1, count):
            total = total + slots[step - 1]
        for copy in copies:
            copy.wait_send()
        return total

    stat[1] = gather(
        stat.at[0], rstat, rsend, rrecv, nrow, lambda step: (lax.rem(row + step, nrow), col)
    )
    summed = gather(
        stat.at[1], cstat, csend, crecv, ncol, lambda step: (row, lax.rem(col + step, ncol))
    )
    grams = jnp.sum(summed, axis=1, keepdims=True)
    g00, g01, g11, g02, g12 = [grams[slot : slot + 1, :] for slot in range(5)]
    alpha = g00 / g01
    norm = alpha * alpha * g11 - 2.0 * alpha * g01 + g00
    beta = norm / (g00 + 1e-06)
    grow = 1.0 + beta
    curve = grow * grow * g01 - grow * alpha * (g02 + g11) + alpha * alpha * g12
    gamma = norm / curve
    sol_ref[...] = (alpha + gamma * grow) * v0[...] - (gamma * alpha) * v1[...]
    res_ref[...] = (
        v0[...] - (alpha + gamma * grow) * v1[...] + (gamma * alpha) * v2[...]
    )
    for condition, copy in pending:
        pl.when(condition)(copy.wait_send)


def shards(measured, denoised, reg_weight, left_blocks, left_cols, right_blocks, right_cols):
    block = left_blocks.shape[-1]
    height, width = measured.shape
    own_rows, own_cols = height // block, width // block
    nrow, ncol = lax.axis_size("row"), lax.axis_size("col")
    halo = 2 * block
    smem = pl.BlockSpec(memory_space=pltpu.SMEM)
    hbm = pl.BlockSpec(memory_space=pltpu.HBM)
    wide, tall = width + 2 * halo, height + 2 * halo
    field = pltpu.VMEM((height, width), F32)
    dma = pltpu.SemaphoreType.DMA
    return pl.pallas_call(
        functools.partial(main_kernel, nrow, ncol, block),
        out_shape=[jax.ShapeDtypeStruct((height, width), F32)] * 2,
        in_specs=[smem] * 3 + [hbm] * 4,
        out_specs=[pl.BlockSpec(memory_space=pltpu.VMEM)] * 2,
        scratch_shapes=[
            field,
            field,
            pltpu.VMEM((2, own_rows + 4, 3, block, block), BF16),
            pltpu.VMEM((2, own_cols + 4, 3, block, block), BF16),
            pltpu.VMEM((2, wide, width), BF16),
            pltpu.VMEM((2, wide, width), BF16),
            pltpu.VMEM((tall, 2 * height), BF16),
            pltpu.VMEM((tall, 2 * height), BF16),
            pltpu.VMEM((OPS, height, width), BF16),
            pltpu.VMEM((OPS, height, halo), BF16),
            pltpu.VMEM((OPS, height, halo), BF16),
            pltpu.VMEM((2 * height, width), BF16),
            pltpu.VMEM((OPS, halo, width), BF16),
            pltpu.VMEM((OPS, halo, width), BF16),
            pltpu.VMEM((OPS, halo, width), BF16),
            pltpu.VMEM((OPS, halo, width), BF16),
            field,
            field,
            field,
            pltpu.VMEM((2, 8, 128), F32),
            pltpu.VMEM((nrow - 1, 8, 128), F32),
            pltpu.VMEM((ncol - 1, 8, 128), F32),
            dma((2,)), dma((2, own_rows + 4)), dma((2, own_cols + 4)),
            dma((OPS, own_rows, 2)), dma((OPS, own_rows, 2)),
            dma((OPS, 2)), dma((OPS, 2)),
            dma((nrow - 1,)), dma((nrow - 1,)), dma((ncol - 1,)), dma((ncol - 1,)),
        ],
        compiler_params=pltpu.CompilerParams(
            collective_id=0, has_side_effects=True, vmem_limit_bytes=48 * 1024 * 1024
        ),
        name="conjugate",
    )(reg_weight, left_cols, right_cols, measured, denoised, left_blocks, right_blocks)


def solution(mesh):
    return jax.shard_map(
        shards,
        mesh=mesh,
        in_specs=(P("row", "col"), P("row", "col"), P(), P(), P(), P(), P()),
        out_specs=(P("row", "col"), P("row", "col")),
        check_vma=False,
    )
```

```python
import functools

import jax
import jax.numpy as jnp
from jax import lax
from jax.experimental import pallas as pl
from jax.experimental.pallas import tpu as pltpu
from jax.sharding import PartitionSpec as P

MESH = pl.DeviceIdType.MESH
BF16 = jnp.bfloat16
F32 = jnp.float32
OPS = 5


def dot(a, b):
    return jnp.dot(a, b, preferred_element_type=F32)


def main_kernel(
    nrow, ncol, block,
    weight_ref, lcols, rcols, meas_hbm, den_hbm, lblk, rblk,
    sol_ref, res_ref,
    meas, den, lwin, rwin, bf_ref, ba_ref, af_ref, aa_ref,
    xo, xl, xr, wo, pu, pd, ru, rd, v0, v1, v2, stat, rstat, cstat,
    msem, lsem, rsem, xsend, xrecv, wsend, wrecv, rsend, rrecv, csend, crecv,
):
    row = lax.axis_index("row")
    col = lax.axis_index("col")
    height, width = meas.shape
    halo = 2 * block
    own_rows, own_cols = height // block, width // block
    nrb, ncb = lblk.shape[1], rblk.shape[1]
    row0, col0 = row * own_rows - 2, col * own_cols - 2
    has_left, has_right = col > 0, col < ncol - 1
    has_up, has_down = row > 0, row < nrow - 1
    left, right = jnp.maximum(col - 1, 0), jnp.minimum(col + 1, ncol - 1)
    up, down = jnp.maximum(row - 1, 0), jnp.minimum(row + 1, nrow - 1)

    load_meas = pltpu.make_async_copy(meas_hbm, meas, msem.at[0])
    load_den = pltpu.make_async_copy(den_hbm, den, msem.at[1])
    load_meas.start()

    def fetch(source, window, sem, first, total, count):
        return [
            pltpu.make_async_copy(
                source.at[k, jnp.clip(first + t, 0, total - 1)], window.at[k, t], sem.at[k, t]
            )
            for k in range(2)
            for t in range(count)
        ]

    load_right = fetch(rblk, rwin, rsem, col0, ncb, own_cols + 4)
    load_left = fetch(lblk, lwin, lsem, row0, nrb, own_rows + 4)
    for copy in load_right:
        copy.start()
    for copy in load_left:
        copy.start()
    load_den.start()

    barrier = pltpu.get_barrier_semaphore()

    @pl.when(jnp.logical_not(has_left))
    def _():
        xl[...] = jnp.zeros_like(xl)

    @pl.when(jnp.logical_not(has_right))
    def _():
        xr[...] = jnp.zeros_like(xr)

    @pl.when(jnp.logical_not(has_up))
    def _():
        ru[...] = jnp.zeros_like(ru)

    @pl.when(jnp.logical_not(has_down))
    def _():
        rd[...] = jnp.zeros_like(rd)

    for step in range(1, nrow):
        pl.semaphore_signal(
            barrier, inc=1, device_id=(lax.rem(row + step, nrow), col), device_id_type=MESH
        )
    for step in range(1, ncol):
        pl.semaphore_signal(
            barrier, inc=1, device_id=(row, lax.rem(col + step, ncol)), device_id_type=MESH
        )
    load_meas.wait()
    xo[0] = meas[...].astype(BF16)
    pl.semaphore_wait(barrier, nrow + ncol - 2)

    def remote(src, dst, send, recv, device):
        return pltpu.make_async_remote_copy(
            src_ref=src, dst_ref=dst, send_sem=send, recv_sem=recv,
            device_id=device, device_id_type=MESH,
        )

    def hit(cols, k, at, total, j, wanted):
        inside = (at >= 0) & (at < total)
        same = cols[k, jnp.clip(at, 0, total - 1), j] == wanted
        return jnp.where(inside & same, 1.0, 0.0).astype(F32)

    def mixed(sources, weights):
        total = sources[0] * weights[0]
        for source, factor in zip(sources[1:], weights[1:]):
            total = total + source * factor
        return total

    def span(index):
        return pl.ds(index * block, block)

    empty = jnp.zeros((block, block), BF16)

    def build_ba():
        for copy in load_right:
            copy.wait()
        for k in range(2):
            for t in range(own_cols + 4):
                sources = [rwin[k, t, j].astype(F32) for j in range(3)]
                for c in range(own_cols):
                    if c <= t <= c + 4:
                        weights = [
                            hit(rcols, k, col0 + t, ncb, j, col0 + 2 + c) for j in range(3)
                        ]
                        ba_ref[k, span(t), span(c)] = mixed(sources, weights).astype(BF16)
                    else:
                        ba_ref[k, span(t), span(c)] = empty

    def build_bf():
        for k in range(2):
            for c in range(own_cols):
                sources = [rwin[k, c + 2, j].astype(F32).T for j in range(3)]
                for t in range(own_cols + 4):
                    if c <= t <= c + 4:
                        weights = [
                            hit(rcols, k, col0 + 2 + c, ncb, j, col0 + t) for j in range(3)
                        ]
                        bf_ref[k, span(t), span(c)] = mixed(sources, weights).astype(BF16)
                    else:
                        bf_ref[k, span(t), span(c)] = empty

    def build_aa():
        for copy in load_left:
            copy.wait()
        for k in range(2):
            for r in range(own_rows):
                sources = [lwin[k, r + 2, j].astype(F32).T for j in range(3)]
                for t in range(own_rows + 4):
                    if r <= t <= r + 4:
                        weights = [
                            hit(lcols, k, row0 + 2 + r, nrb, j, row0 + t) for j in range(3)
                        ]
                        value = mixed(sources, weights).astype(BF16)
                    else:
                        value = empty
                    aa_ref[span(t), span(k * own_rows + r)] = value

    def build_af():
        for k in range(2):
            for t in range(own_rows + 4):
                sources = [lwin[k, t, j].astype(F32) for j in range(3)]
                for r in range(own_rows):
                    if r <= t <= r + 4:
                        weights = [
                            hit(lcols, k, row0 + t, nrb, j, row0 + 2 + r) for j in range(3)
                        ]
                        value = mixed(sources, weights).astype(BF16)
                    else:
                        value = empty
                    af_ref[span(t), span(k * own_rows + r)] = value

    pending = []
    chunks = range(own_rows)

    def operate(index, bmat, amat, fill_b=None, fill_a=None):
        sides = []
        for q in chunks:
            to_right = remote(
                xo.at[index, span(q), pl.ds(width - halo, halo)], xl.at[index, span(q)],
                xsend.at[index, q, 0], xrecv.at[index, q, 0], (row, right),
            )
            to_left = remote(
                xo.at[index, span(q), pl.ds(0, halo)], xr.at[index, span(q)],
                xsend.at[index, q, 1], xrecv.at[index, q, 1], (row, left),
            )
            pl.when(has_right)(to_right.start)
            pl.when(has_left)(to_left.start)
            pending.append((has_right, to_right))
            pending.append((has_left, to_left))
            sides.append((to_right, to_left))
        if fill_b is not None:
            fill_b()
        acc = [dot(xo[index], bmat[k, pl.ds(halo, width), :]) for k in range(2)]
        for q in chunks:
            to_right, to_left = sides[q]
            pl.when(has_left)(to_right.wait_recv)
            pl.when(has_right)(to_left.wait_recv)
            for k in range(2):
                total = acc[k][q * block : (q + 1) * block]
                total = total + dot(xl[index, span(q)], bmat[k, pl.ds(0, halo), :])
                total = total + dot(xr[index, span(q)], bmat[k, pl.ds(halo + width, halo), :])
                wo[span(k * own_rows + q)] = total.astype(BF16)
        if fill_a is not None:
            fill_a()
        products = wo[...]
        to_down = remote(
            pd.at[index], ru.at[index], wsend.at[index, 0], wrecv.at[index, 0], (down, col)
        )
        to_up = remote(
            pu.at[index], rd.at[index], wsend.at[index, 1], wrecv.at[index, 1], (up, col)
        )
        pd[index] = dot(amat[pl.ds(halo + height, halo), :], products).astype(BF16)
        pl.when(has_down)(to_down.start)
        pu[index] = dot(amat[pl.ds(0, halo), :], products).astype(BF16)
        pl.when(has_up)(to_up.start)
        pending.append((has_down, to_down))
        pending.append((has_up, to_up))
        out = dot(amat[pl.ds(halo, height), :], products)
        pl.when(has_up)(to_down.wait_recv)
        pl.when(has_down)(to_up.wait_recv)
        return out + ru[index].astype(F32) + rd[index].astype(F32)

    weight = weight_ref[0]
    first = operate(0, ba_ref, aa_ref, build_ba, build_aa)
    load_den.wait()
    first = first + weight * den[...]
    xo[1] = first.astype(BF16)
    v0[...] = first
    xo[2] = operate(1, bf_ref, af_ref, build_bf, build_af).astype(BF16)
    second = operate(2, ba_ref, aa_ref) + weight * v0[...]
    xo[3] = second.astype(BF16)
    v1[...] = second
    xo[4] = operate(3, bf_ref, af_ref).astype(BF16)
    v2[...] = operate(4, ba_ref, aa_ref) + weight * v1[...]

    def lanes(a, b):
        folded = jnp.sum(a[...] * b[...], axis=0, keepdims=True)
        total = folded[:, 0:128]
        for start in range(128, width, 128):
            total = total + folded[:, start : start + 128]
        return total

    for slot, (a, b) in enumerate(((v0, v0), (v0, v1), (v1, v1), (v0, v2), (v1, v2))):
        stat[0, pl.ds(slot, 1), :] = lanes(a, b)
    stat[0, pl.ds(5, 3), :] = jnp.zeros((3, 128), F32)

    def gather(source, slots, send, recv, count, device):
        copies = [
            remote(source, slots.at[step - 1], send.at[step - 1], recv.at[step - 1], device(step))
            for step in range(1, count)
        ]
        for copy in copies:
            copy.start()
        for copy in copies:
            copy.wait_recv()
        total = source[...]
        for step in range(1, count):
            total = total + slots[step - 1]
        for copy in copies:
            copy.wait_send()
        return total

    stat[1] = gather(
        stat.at[0], rstat, rsend, rrecv, nrow, lambda step: (lax.rem(row + step, nrow), col)
    )
    summed = gather(
        stat.at[1], cstat, csend, crecv, ncol, lambda step: (row, lax.rem(col + step, ncol))
    )
    grams = jnp.sum(summed, axis=1, keepdims=True)
    g00, g01, g11, g02, g12 = [grams[slot : slot + 1, :] for slot in range(5)]
    alpha = g00 / g01
    norm = alpha * alpha * g11 - 2.0 * alpha * g01 + g00
    beta = norm / (g00 + 1e-06)
    grow = 1.0 + beta
    curve = grow * grow * g01 - grow * alpha * (g02 + g11) + alpha * alpha * g12
    gamma = norm / curve
    sol_ref[...] = (alpha + gamma * grow) * v0[...] - (gamma * alpha) * v1[...]
    res_ref[...] = (
        v0[...] - (alpha + gamma * grow) * v1[...] + (gamma * alpha) * v2[...]
    )
    for condition, copy in pending:
        pl.when(condition)(copy.wait_send)


def shards(measured, denoised, reg_weight, left_blocks, left_cols, right_blocks, right_cols):
    block = left_blocks.shape[-1]
    height, width = measured.shape
    own_rows, own_cols = height // block, width // block
    nrow, ncol = lax.axis_size("row"), lax.axis_size("col")
    halo = 2 * block
    smem = pl.BlockSpec(memory_space=pltpu.SMEM)
    hbm = pl.BlockSpec(memory_space=pltpu.HBM)
    wide, tall = width + 2 * halo, height + 2 * halo
    field = pltpu.VMEM((height, width), F32)
    dma = pltpu.SemaphoreType.DMA
    return pl.pallas_call(
        functools.partial(main_kernel, nrow, ncol, block),
        out_shape=[jax.ShapeDtypeStruct((height, width), F32)] * 2,
        in_specs=[smem] * 3 + [hbm] * 4,
        out_specs=[pl.BlockSpec(memory_space=pltpu.VMEM)] * 2,
        scratch_shapes=[
            field,
            field,
            pltpu.VMEM((2, own_rows + 4, 3, block, block), BF16),
            pltpu.VMEM((2, own_cols + 4, 3, block, block), BF16),
            pltpu.VMEM((2, wide, width), BF16),
            pltpu.VMEM((2, wide, width), BF16),
            pltpu.VMEM((tall, 2 * height), BF16),
            pltpu.VMEM((tall, 2 * height), BF16),
            pltpu.VMEM((OPS, height, width), BF16),
            pltpu.VMEM((OPS, height, halo), BF16),
            pltpu.VMEM((OPS, height, halo), BF16),
            pltpu.VMEM((2 * height, width), BF16),
            pltpu.VMEM((OPS, halo, width), BF16),
            pltpu.VMEM((OPS, halo, width), BF16),
            pltpu.VMEM((OPS, halo, width), BF16),
            pltpu.VMEM((OPS, halo, width), BF16),
            field,
            field,
            field,
            pltpu.VMEM((2, 8, 128), F32),
            pltpu.VMEM((nrow - 1, 8, 128), F32),
            pltpu.VMEM((ncol - 1, 8, 128), F32),
            dma((2,)), dma((2, own_rows + 4)), dma((2, own_cols + 4)),
            dma((OPS, own_rows, 2)), dma((OPS, own_rows, 2)),
            dma((OPS, 2)), dma((OPS, 2)),
            dma((nrow - 1,)), dma((nrow - 1,)), dma((ncol - 1,)), dma((ncol - 1,)),
        ],
        compiler_params=pltpu.CompilerParams(
            collective_id=0, has_side_effects=True, vmem_limit_bytes=60 * 1024 * 1024
        ),
        name="conjugate",
    )(reg_weight, left_cols, right_cols, measured, denoised, left_blocks, right_blocks)


def solution(mesh):
    return jax.shard_map(
        shards,
        mesh=mesh,
        in_specs=(P("row", "col"), P("row", "col"), P(), P(), P(), P(), P()),
        out_specs=(P("row", "col"), P("row", "col")),
        check_vma=False,
    )
```

```python
import functools

import jax
import jax.numpy as jnp
from jax import lax
from jax.experimental import pallas as pl
from jax.experimental.pallas import tpu as pltpu
from jax.sharding import PartitionSpec as P

MESH = pl.DeviceIdType.MESH
BF16 = jnp.bfloat16
F32 = jnp.float32
OPS = 5


def dot(a, b):
    return jnp.dot(a, b, preferred_element_type=F32)


def main_kernel(
    nrow, ncol, block,
    weight_ref, lcols_hbm, rcols_hbm, meas_hbm, den_hbm, lblk, rblk,
    sol_ref, res_ref,
    lcols, rcols, meas, den, lwin, rwin, bf_ref, ba_ref, af_ref, aa_ref,
    xo, xl, xr, wo, pu, pd, ru, rd, v0, v1, v2, stat, rstat, cstat,
    msem, lsem, rsem, xsend, xrecv, wsend, wrecv, rsend, rrecv, csend, crecv,
):
    row = lax.axis_index("row")
    col = lax.axis_index("col")
    height, width = meas.shape
    halo = 2 * block
    own_rows, own_cols = height // block, width // block
    nrb, ncb = lblk.shape[1], rblk.shape[1]
    row0, col0 = row * own_rows - 2, col * own_cols - 2
    has_left, has_right = col > 0, col < ncol - 1
    has_up, has_down = row > 0, row < nrow - 1
    left, right = jnp.maximum(col - 1, 0), jnp.minimum(col + 1, ncol - 1)
    up, down = jnp.maximum(row - 1, 0), jnp.minimum(row + 1, nrow - 1)

    load_meas = pltpu.make_async_copy(meas_hbm, meas, msem.at[0])
    load_den = pltpu.make_async_copy(den_hbm, den, msem.at[1])
    load_meas.start()
    load_lcols = pltpu.make_async_copy(lcols_hbm, lcols, msem.at[2])
    load_rcols = pltpu.make_async_copy(rcols_hbm, rcols, msem.at[3])
    load_lcols.start()
    load_rcols.start()

    def fetch(source, window, sem, first, total, count):
        return [
            pltpu.make_async_copy(
                source.at[k, jnp.clip(first + t, 0, total - 1)], window.at[k, t], sem.at[k, t]
            )
            for k in range(2)
            for t in range(count)
        ]

    load_right = fetch(rblk, rwin, rsem, col0, ncb, own_cols + 4)
    load_left = fetch(lblk, lwin, lsem, row0, nrb, own_rows + 4)
    for copy in load_right:
        copy.start()
    for copy in load_left:
        copy.start()
    load_den.start()

    barrier = pltpu.get_barrier_semaphore()

    @pl.when(jnp.logical_not(has_left))
    def _():
        xl[...] = jnp.zeros_like(xl)

    @pl.when(jnp.logical_not(has_right))
    def _():
        xr[...] = jnp.zeros_like(xr)

    @pl.when(jnp.logical_not(has_up))
    def _():
        ru[...] = jnp.zeros_like(ru)

    @pl.when(jnp.logical_not(has_down))
    def _():
        rd[...] = jnp.zeros_like(rd)

    for step in range(1, nrow):
        pl.semaphore_signal(
            barrier, inc=1, device_id=(lax.rem(row + step, nrow), col), device_id_type=MESH
        )
    for step in range(1, ncol):
        pl.semaphore_signal(
            barrier, inc=1, device_id=(row, lax.rem(col + step, ncol)), device_id_type=MESH
        )
    load_meas.wait()
    xo[0] = meas[...].astype(BF16)
    pl.semaphore_wait(barrier, nrow + ncol - 2)

    def remote(src, dst, send, recv, device):
        return pltpu.make_async_remote_copy(
            src_ref=src, dst_ref=dst, send_sem=send, recv_sem=recv,
            device_id=device, device_id_type=MESH,
        )

    def hit(cols, k, at, total, j, wanted):
        inside = (at >= 0) & (at < total)
        same = cols[k, jnp.clip(at, 0, total - 1), j] == wanted
        return jnp.where(inside & same, 1.0, 0.0).astype(F32)

    def mixed(sources, weights):
        total = sources[0] * weights[0]
        for source, factor in zip(sources[1:], weights[1:]):
            total = total + source * factor
        return total

    def span(index):
        return pl.ds(index * block, block)

    empty = jnp.zeros((block, block), BF16)

    def build_ba():
        load_rcols.wait()
        for copy in load_right:
            copy.wait()
        for k in range(2):
            for t in range(own_cols + 4):
                sources = [rwin[k, t, j].astype(F32) for j in range(3)]
                for c in range(own_cols):
                    if c <= t <= c + 4:
                        weights = [
                            hit(rcols, k, col0 + t, ncb, j, col0 + 2 + c) for j in range(3)
                        ]
                        ba_ref[k, span(t), span(c)] = mixed(sources, weights).astype(BF16)
                    else:
                        ba_ref[k, span(t), span(c)] = empty

    def build_bf():
        for k in range(2):
            for c in range(own_cols):
                sources = [rwin[k, c + 2, j].astype(F32).T for j in range(3)]
                for t in range(own_cols + 4):
                    if c <= t <= c + 4:
                        weights = [
                            hit(rcols, k, col0 + 2 + c, ncb, j, col0 + t) for j in range(3)
                        ]
                        bf_ref[k, span(t), span(c)] = mixed(sources, weights).astype(BF16)
                    else:
                        bf_ref[k, span(t), span(c)] = empty

    def build_aa():
        load_lcols.wait()
        for copy in load_left:
            copy.wait()
        for k in range(2):
            for r in range(own_rows):
                sources = [lwin[k, r + 2, j].astype(F32).T for j in range(3)]
                for t in range(own_rows + 4):
                    if r <= t <= r + 4:
                        weights = [
                            hit(lcols, k, row0 + 2 + r, nrb, j, row0 + t) for j in range(3)
                        ]
                        value = mixed(sources, weights).astype(BF16)
                    else:
                        value = empty
                    aa_ref[span(t), span(k * own_rows + r)] = value

    def build_af():
        for k in range(2):
            for t in range(own_rows + 4):
                sources = [lwin[k, t, j].astype(F32) for j in range(3)]
                for r in range(own_rows):
                    if r <= t <= r + 4:
                        weights = [
                            hit(lcols, k, row0 + t, nrb, j, row0 + 2 + r) for j in range(3)
                        ]
                        value = mixed(sources, weights).astype(BF16)
                    else:
                        value = empty
                    af_ref[span(t), span(k * own_rows + r)] = value

    pending = []
    chunks = range(own_rows)

    def operate(index, bmat, amat, fill_b=None, fill_a=None):
        sides = []
        for q in chunks:
            to_right = remote(
                xo.at[index, span(q), pl.ds(width - halo, halo)], xl.at[index, span(q)],
                xsend.at[index, q, 0], xrecv.at[index, q, 0], (row, right),
            )
            to_left = remote(
                xo.at[index, span(q), pl.ds(0, halo)], xr.at[index, span(q)],
                xsend.at[index, q, 1], xrecv.at[index, q, 1], (row, left),
            )
            pl.when(has_right)(to_right.start)
            pl.when(has_left)(to_left.start)
            pending.append((has_right, to_right))
            pending.append((has_left, to_left))
            sides.append((to_right, to_left))
        if fill_b is not None:
            fill_b()
        acc = [dot(xo[index], bmat[k, pl.ds(halo, width), :]) for k in range(2)]
        for q in chunks:
            to_right, to_left = sides[q]
            near = [acc[k][q * block : (q + 1) * block] for k in range(2)]
            pl.when(has_left)(to_right.wait_recv)
            for k in range(2):
                near[k] = near[k] + dot(xl[index, span(q)], bmat[k, pl.ds(0, halo), :])
            pl.when(has_right)(to_left.wait_recv)
            for k in range(2):
                total = near[k] + dot(xr[index, span(q)], bmat[k, pl.ds(halo + width, halo), :])
                wo[span(k * own_rows + q)] = total.astype(BF16)
        if fill_a is not None:
            fill_a()
        products = wo[...]
        to_down = remote(
            pd.at[index], ru.at[index], wsend.at[index, 0], wrecv.at[index, 0], (down, col)
        )
        to_up = remote(
            pu.at[index], rd.at[index], wsend.at[index, 1], wrecv.at[index, 1], (up, col)
        )
        pd[index] = dot(amat[pl.ds(halo + height, halo), :], products).astype(BF16)
        pl.when(has_down)(to_down.start)
        pu[index] = dot(amat[pl.ds(0, halo), :], products).astype(BF16)
        pl.when(has_up)(to_up.start)
        pending.append((has_down, to_down))
        pending.append((has_up, to_up))
        out = dot(amat[pl.ds(halo, height), :], products)
        pl.when(has_up)(to_down.wait_recv)
        pl.when(has_down)(to_up.wait_recv)
        return out + ru[index].astype(F32) + rd[index].astype(F32)

    def lanes(a, b):
        folded = jnp.sum(a[...] * b[...], axis=0, keepdims=True)
        total = folded[:, 0:128]
        for start in range(128, width, 128):
            total = total + folded[:, start : start + 128]
        return total

    def products_from(pairs, first_slot):
        for slot, (a, b) in enumerate(pairs):
            stat[0, pl.ds(first_slot + slot, 1), :] = lanes(a, b)

    def early():
        products_from(((v0, v0), (v0, v1), (v1, v1)), 0)
        stat[0, pl.ds(5, 3), :] = jnp.zeros((3, 128), F32)

    weight = weight_ref[0]
    first = operate(0, ba_ref, aa_ref, build_ba, build_aa)
    load_den.wait()
    first = first + weight * den[...]
    xo[1] = first.astype(BF16)
    v0[...] = first
    xo[2] = operate(1, bf_ref, af_ref, build_bf, build_af).astype(BF16)
    second = operate(2, ba_ref, aa_ref) + weight * v0[...]
    xo[3] = second.astype(BF16)
    v1[...] = second
    xo[4] = operate(3, bf_ref, af_ref).astype(BF16)
    v2[...] = operate(4, ba_ref, aa_ref, early) + weight * v1[...]

    products_from(((v0, v2), (v1, v2)), 3)

    def gather(source, slots, send, recv, count, device):
        copies = [
            remote(source, slots.at[step - 1], send.at[step - 1], recv.at[step - 1], device(step))
            for step in range(1, count)
        ]
        for copy in copies:
            copy.start()
        for copy in copies:
            copy.wait_recv()
        total = source[...]
        for step in range(1, count):
            total = total + slots[step - 1]
        for copy in copies:
            copy.wait_send()
        return total

    stat[1] = gather(
        stat.at[0], rstat, rsend, rrecv, nrow, lambda step: (lax.rem(row + step, nrow), col)
    )
    summed = gather(
        stat.at[1], cstat, csend, crecv, ncol, lambda step: (row, lax.rem(col + step, ncol))
    )
    grams = jnp.sum(summed, axis=1, keepdims=True)
    g00, g01, g11, g02, g12 = [grams[slot : slot + 1, :] for slot in range(5)]
    alpha = g00 / g01
    norm = alpha * alpha * g11 - 2.0 * alpha * g01 + g00
    beta = norm / (g00 + 1e-06)
    grow = 1.0 + beta
    curve = grow * grow * g01 - grow * alpha * (g02 + g11) + alpha * alpha * g12
    gamma = norm / curve
    sol_ref[...] = (alpha + gamma * grow) * v0[...] - (gamma * alpha) * v1[...]
    res_ref[...] = (
        v0[...] - (alpha + gamma * grow) * v1[...] + (gamma * alpha) * v2[...]
    )
    for condition, copy in pending:
        pl.when(condition)(copy.wait_send)


def shards(measured, denoised, reg_weight, left_blocks, left_cols, right_blocks, right_cols):
    block = left_blocks.shape[-1]
    height, width = measured.shape
    own_rows, own_cols = height // block, width // block
    nrow, ncol = lax.axis_size("row"), lax.axis_size("col")
    halo = 2 * block
    smem = pl.BlockSpec(memory_space=pltpu.SMEM)
    hbm = pl.BlockSpec(memory_space=pltpu.HBM)
    wide, tall = width + 2 * halo, height + 2 * halo
    field = pltpu.VMEM((height, width), F32)
    dma = pltpu.SemaphoreType.DMA
    return pl.pallas_call(
        functools.partial(main_kernel, nrow, ncol, block),
        out_shape=[jax.ShapeDtypeStruct((height, width), F32)] * 2,
        in_specs=[smem] + [hbm] * 6,
        out_specs=[pl.BlockSpec(memory_space=pltpu.VMEM)] * 2,
        scratch_shapes=[
            pltpu.SMEM(left_cols.shape, jnp.int32),
            pltpu.SMEM(right_cols.shape, jnp.int32),
            field,
            field,
            pltpu.VMEM((2, own_rows + 4, 3, block, block), BF16),
            pltpu.VMEM((2, own_cols + 4, 3, block, block), BF16),
            pltpu.VMEM((2, wide, width), BF16),
            pltpu.VMEM((2, wide, width), BF16),
            pltpu.VMEM((tall, 2 * height), BF16),
            pltpu.VMEM((tall, 2 * height), BF16),
            pltpu.VMEM((OPS, height, width), BF16),
            pltpu.VMEM((OPS, height, halo), BF16),
            pltpu.VMEM((OPS, height, halo), BF16),
            pltpu.VMEM((2 * height, width), BF16),
            pltpu.VMEM((OPS, halo, width), BF16),
            pltpu.VMEM((OPS, halo, width), BF16),
            pltpu.VMEM((OPS, halo, width), BF16),
            pltpu.VMEM((OPS, halo, width), BF16),
            field,
            field,
            field,
            pltpu.VMEM((2, 8, 128), F32),
            pltpu.VMEM((nrow - 1, 8, 128), F32),
            pltpu.VMEM((ncol - 1, 8, 128), F32),
            dma((4,)), dma((2, own_rows + 4)), dma((2, own_cols + 4)),
            dma((OPS, own_rows, 2)), dma((OPS, own_rows, 2)),
            dma((OPS, 2)), dma((OPS, 2)),
            dma((nrow - 1,)), dma((nrow - 1,)), dma((ncol - 1,)), dma((ncol - 1,)),
        ],
        compiler_params=pltpu.CompilerParams(
            collective_id=0, has_side_effects=True, vmem_limit_bytes=60 * 1024 * 1024
        ),
        name="conjugate",
    )(reg_weight, left_cols, right_cols, measured, denoised, left_blocks, right_blocks)


def solution(mesh):
    return jax.shard_map(
        shards,
        mesh=mesh,
        in_specs=(P("row", "col"), P("row", "col"), P(), P(), P(), P(), P()),
        out_specs=(P("row", "col"), P("row", "col")),
        check_vma=False,
    )
```
